32 devices in a mesh: section: 4 (over x, core), ep: 8 (over z, y).
Axes of the slice: x: 2, y: 2, z: 4, core: 2. Of those that a mesh axis runs over, the one named last changes fastest.
Arguments:
- hidden: bfloat16 [1024, 4096], P(('section', 'ep')), may hold values from -6 to 6
- route_ids: int32 [4, 1024, 8], P(None, ('section', 'ep')), may hold values from 0 to 127, all different within a row; in each aligned block of 32 rows (0 to 31, 32 to 63, ..., all dimensions but the last counted through in order) at most 4 rows name the same one
- route_logits: float32 [4, 1024, 8], P(None, ('section', 'ep')), may hold values from -4 to 4
- norm_gain: bfloat16 [4, 4096], P('section'), may hold values from 0.099609375 to 1.8984375
- w_gate: bfloat16 [4, 3072, 4096], P('section', 'ep'), may hold values from -0.09375 to 0.09375
- w_up: bfloat16 [4, 3072, 4096], P('section', 'ep'), may hold values from -0.09375 to 0.09375
- w_down: bfloat16 [4, 3072, 4096], P('section', 'ep'), may hold values from -0.625 to 0.625
Outputs:
- final_hidden: bfloat16 [1024, 4096], P(('section', 'ep'))
The draws below stay inside these ranges and needn't reach their ends.
Inputs may be any that keep to these rules, and one draw needn't show every extreme that they name: `route_ids`: in each tick, at most 4 of the 32 rows of one device name any one expert; each row names 8 different experts.
All inputs are finite; a program needn't handle non-finite values.
Results may differ from the reference program's by a relative error of at most 0.0043.
Values may be sent and summed in bfloat16 or wider, within the bound.
A program may use at most 64 MiB of HBM per device.

```python
import math
import jax
import jax.numpy as jnp
import numpy as np
from jax import lax

D = 4096
FE = 1536
EXPERTS = 128
TOP = 8
MOST = 4
TICKS = 4
ROWS_DEV = 32
HELD = 2
ROWS_ST = 256
ROWS_ALL = 1024
N_SECTION = 4
N_EP = 8


def shard_levels(key, shape, shards, least, top_value):
    def one(axis_at, shards_of):
        steps = jax.random.uniform(jax.random.fold_in(jax.random.fold_in(key, 6), axis_at), (shards_of,), jnp.float32, least / len(shards), top_value / len(shards))
        return jnp.repeat(jnp.exp(steps), shape[axis_at] // shards_of).reshape((-1,) + (1,) * (len(shape) - axis_at - 1))

    factor_of = one(*shards[0])
    for cut in shards[1:]:
        factor_of = factor_of * one(*cut)
    return factor_of


def assign_block(key, own, number, rows, count, top, bound, lean):
    sequence = jax.random.permutation(key, count)
    heavy_load, ordinary = portions_of(count, rows * top, bound, lean, True), portions_of(count, rows * top, bound, lean, False)
    places = jnp.arange(count)

    def named(tallies, offset_by):
        used = int((tallies > 0).sum())
        fixed = max(1, used // 4)
        shifted = fixed + (places - fixed + offset_by * (used - fixed)) % max(1, count - fixed)
        return jnp.zeros((count,), jnp.int32).at[sequence[jnp.where(places < fixed, places, shifted)]].set(jnp.asarray(tallies, jnp.int32))

    tallies = jnp.where(number % 4 == 0, named(heavy_load, number // 4), named(ordinary, number - number // 4 - 1))
    mixed = jax.random.permutation(jax.random.fold_in(own, 3), count)
    donor, sink = mixed[0:count // 2 * 2:2], mixed[1:count // 2 * 2:2]
    margin = jnp.minimum(tallies[donor] - 1, bound - tallies[sink]) // 2
    margin = jnp.where((donor == sequence[0]) | (sink == sequence[0]) | (tallies[sink] == 0), 0, jnp.maximum(margin, 0))
    shifted = jax.random.randint(jax.random.fold_in(own, 4), (count // 2,), 0, 1 << 20) % (margin + 1)
    tallies = tallies.at[donor].add(-shifted).at[sink].add(shifted)
    labels = jnp.searchsorted(jnp.cumsum(tallies), jnp.arange(rows * top), side="right").astype(jnp.int32)
    table = labels.reshape(top, rows).T
    table = table[jax.random.permutation(jax.random.fold_in(own, 1), rows)]
    offset_by = jax.random.randint(jax.random.fold_in(own, 2), (rows, 1), 0, top)
    return jnp.take_along_axis(table, (jnp.arange(top)[None, :] + offset_by) % top, axis=1)


def portions_of(amount, total, limit, slope, full):
    loads = [(1 << 20) // math.isqrt(rank ** slope) + 1 for rank in range(1, amount + 1)]
    largest = limit if full else min(limit, max(-(-total // amount), total * loads[0] // sum(loads)))
    least = 1 if total - largest >= amount - 1 else 0
    given, surplus = [largest] + [least] * (amount - 1), total - largest - least * (amount - 1)
    while surplus > 0:
        movable = [i for i in range(1, amount) if given[i] < largest] or [i for i in range(1, amount) if given[i] < limit]
        whole, left = sum([loads[i] for i in movable]), surplus
        for i in movable:
            addition = min(limit - given[i], max(1, left * loads[i] // whole), surplus)
            given[i] = given[i] + addition
            surplus = surplus - addition
    return np.array(given)


def scatter_about(key, extent, scale, most, pieces=(), kind=jnp.bfloat16):
    loudness = shard_levels(key, extent, pieces, -0.22, 0.18) if pieces else 1.0
    values = jax.random.normal(key, extent, jnp.float32) * scale * loudness
    return jnp.minimum(jnp.maximum(values, -most), most).astype(kind)


def setup_inputs(seed: int = 0) -> dict:
    key_of = jax.random.split(jax.random.key(seed), 8)
    hidden = scatter_about(key_of[0], (ROWS_ALL, D), 1.0, 6.0, ((0, 32),))
    route_ids_keys = jax.random.split(jax.random.fold_in(key_of[1], 1), TICKS * ROWS_ALL // ROWS_DEV)
    route_ids_turns = jax.random.permutation(jax.random.fold_in(key_of[1], 3), TICKS * ROWS_ALL // ROWS_DEV)
    route_ids = jax.vmap(lambda own, number: assign_block(jax.random.fold_in(key_of[1], 2), own, number, ROWS_DEV, EXPERTS, TOP, MOST, 2))(route_ids_keys, route_ids_turns).reshape((TICKS, ROWS_ALL, TOP))
    route_logits = scatter_about(key_of[2], (TICKS, ROWS_ALL, TOP), 1.0, 4.0, ((1, 32),), jnp.float32)
    norm_gain = jnp.clip(1.0 + 0.18 * jax.random.normal(key_of[3], (N_SECTION, D), jnp.float32), 0.099609375, 1.8984375).astype(jnp.bfloat16)
    w_gate = scatter_about(key_of[4], (N_SECTION, HELD * FE, D), D ** -0.5, 0.09375, ((0, 4), (1, 8)))
    w_up = scatter_about(key_of[5], (N_SECTION, HELD * FE, D), D ** -0.5, 0.09375, ((0, 4), (1, 8)))
    w_down = scatter_about(key_of[6], (N_SECTION, HELD * FE, D), (FE // 16) ** -0.5, 0.625, ((0, 4), (1, 8)))
    return dict(hidden=hidden, route_ids=route_ids, route_logits=route_logits, norm_gain=norm_gain, w_gate=w_gate, w_up=w_up, w_down=w_down)


def project_rows(rows, weight_t):
    return lax.dot_general(rows, weight_t, (((1,), (1,)), ((), ())), preferred_element_type=jnp.float32)

def expert_out(rows, wg, wu, wd):
    gate = project_rows(rows, wg)
    upper = project_rows(rows, wu)
    act = (jax.nn.silu(gate) * upper).astype(jnp.bfloat16)
    return jnp.dot(act, wd, preferred_element_type=jnp.float32)

def segment_step(args):
    h, ids, logits, gain, wg, wu, wd = args
    wg3 = wg.reshape(HELD, FE, D)
    wu3 = wu.reshape(HELD, FE, D)
    wd3 = wd.reshape(HELD, FE, D)
    hf = h.astype(jnp.float32)
    msq = lax.optimization_barrier(jnp.mean(hf * hf, axis=-1, keepdims=True)) + 1e-06
    normed = (hf * lax.rsqrt(msq) * gain.astype(jnp.float32)).astype(jnp.bfloat16)
    expo = jnp.exp(logits)
    probs = expo / lax.optimization_barrier(jnp.sum(expo, axis=-1, keepdims=True))
    out = hf
    for j in range(HELD):
        match = ids == j
        weight = lax.optimization_barrier(jnp.sum(jnp.where(match, probs, 0.0), axis=-1)).astype(jnp.bfloat16)
        hits = jnp.any(match, axis=-1).astype(jnp.int32).reshape(N_EP, ROWS_DEV)
        order = jnp.argsort(1 - hits, axis=1, stable=True)[:, :MOST].astype(jnp.int32)
        count = lax.optimization_barrier(jnp.sum(hits, axis=1))
        valid = jnp.arange(MOST, dtype=jnp.int32)[None, :] < count[:, None]
        picks = (order + jnp.arange(N_EP, dtype=jnp.int32)[:, None] * ROWS_DEV).reshape(-1)
        slot_w = jnp.where(valid.reshape(-1), weight[picks], jnp.zeros((), jnp.bfloat16))
        y_rows = expert_out(normed[picks], wg3[j], wu3[j], wd3[j])
        out = out.at[picks].add(slot_w.astype(jnp.float32)[:, None] * y_rows)
    return out.astype(jnp.bfloat16)

def reference(hidden, route_ids, route_logits, norm_gain, w_gate, w_up, w_down):
    state = hidden.reshape(N_SECTION, ROWS_ST, D)
    for tick in range(TICKS):
        ids = route_ids[tick].reshape(N_SECTION, ROWS_ST, TOP)
        logits = route_logits[tick].reshape(N_SECTION, ROWS_ST, TOP)
        fresh = lax.map(segment_step, (state, ids, logits, norm_gain, w_gate, w_up, w_down))
        state = jnp.roll(fresh, 1, axis=0)
    return state.reshape(ROWS_ALL, D)
```

```python
import functools

import jax
import jax.numpy as jnp
from jax import lax
from jax.experimental import pallas as pl
from jax.experimental.pallas import tpu as pltpu
from jax.sharding import PartitionSpec as P

FE = 1536
MOST = 4
MESH = pl.DeviceIdType.MESH


def nt_dot(rows, weight_t):
    return lax.dot_general(
        rows, weight_t, (((1,), (1,)), ((), ())), preferred_element_type=jnp.float32
    )


def kernel(
    sections,
    peers,
    sharers,
    ids_ref,
    logits_ref,
    gain_ref,
    hidden_ref,
    wg_hbm,
    wu_hbm,
    wd_hbm,
    out_ref,
    wg,
    wu,
    wd,
    state,
    held_h,
    send_a,
    recv_a,
    send_b,
    recv_b,
    pick,
    comb,
    comb_prev,
    rows_f,
    y_f,
    w_sem,
    sa_sem,
    ra_sem,
    sb_sem,
    rb_sem,
    sh_sem,
    rh_sem,
    c_sem,
    own_sem,
):
    ticks, rows_dev, top = ids_ref.shape
    held = peers // sharers
    sec = lax.axis_index("section")
    me = lax.axis_index("ep")
    after = lax.rem(sec + 1, sections)
    before = lax.rem(sec + sections - 1, sections)

    loads = [
        pltpu.make_async_copy(src, dst, w_sem.at[i])
        for i, (src, dst) in enumerate(((wg_hbm, wg), (wu_hbm, wu), (wd_hbm, wd)))
    ]
    for load in loads:
        load.start()

    barrier = pltpu.get_barrier_semaphore()
    for k in range(peers):
        other = lax.rem(me + k, peers)
        if k:
            pl.semaphore_signal(barrier, inc=1, device_id=(sec, other), device_id_type=MESH)
        pl.semaphore_signal(barrier, inc=1, device_id=(before, other), device_id_type=MESH)

    tri = (
        lax.broadcasted_iota(jnp.int32, (rows_dev, rows_dev), 1)
        < lax.broadcasted_iota(jnp.int32, (rows_dev, rows_dev), 0)
    ).astype(jnp.bfloat16)
    lane = lax.broadcasted_iota(jnp.int32, (rows_dev, 128), 1)
    eye = (
        lax.broadcasted_iota(jnp.int32, (held * MOST, 128), 0) * 1
    )
    eye_row = eye // MOST * (sharers * MOST) + eye % MOST
    eye_bf = (lax.broadcasted_iota(jnp.int32, (held * MOST, 128), 1) == eye_row).astype(
        jnp.bfloat16
    )
    for t in range(ticks):
        ids = ids_ref[t]
        expo = jnp.exp(logits_ref[t])
        probs = expo / jnp.sum(expo, axis=-1, keepdims=True)
        hits = jnp.zeros((rows_dev, 128), jnp.float32)
        weights = jnp.zeros((rows_dev, 128), jnp.float32)
        for j in range(held):
            match = ids == j
            hit = jnp.sum(jnp.where(match, 1.0, 0.0), axis=-1, keepdims=True)
            weight = jnp.sum(jnp.where(match, probs, 0.0), axis=-1, keepdims=True)
            mine = lane // (sharers * MOST) == j
            hits = jnp.where(mine, hit, hits)
            weights = jnp.where(mine, weight, weights)
        place = jnp.dot(tri, hits.astype(jnp.bfloat16), preferred_element_type=jnp.float32)
        slot = lax.rem(lane, MOST).astype(jnp.float32)
        chosen = jnp.where(place == slot, hits, 0.0)
        comb[t] = (chosen * weights.astype(jnp.bfloat16).astype(jnp.float32)).astype(jnp.bfloat16)
        pick[t] = nt_dot(eye_bf, chosen.astype(jnp.bfloat16)).astype(jnp.bfloat16)

    state[0] = hidden_ref[...]
    pl.semaphore_wait(barrier, 2 * peers - 1)
    comb_copy = pltpu.make_async_remote_copy(
        src_ref=comb,
        dst_ref=comb_prev,
        send_sem=c_sem.at[0],
        recv_sem=c_sem.at[1],
        device_id=(after, me),
        device_id_type=MESH,
    )
    comb_copy.start()

    def copy_a(t, k):
        other = lax.rem(me + k, peers)
        return pltpu.make_async_remote_copy(
            src_ref=send_a.at[t, other // sharers],
            dst_ref=recv_a.at[t, me],
            send_sem=sa_sem.at[t, k],
            recv_sem=ra_sem.at[t, k],
            device_id=(sec, other),
            device_id_type=MESH,
        )

    def copy_b(t, k):
        other = lax.rem(me + k, peers)
        return pltpu.make_async_remote_copy(
            src_ref=send_b.at[t, other],
            dst_ref=recv_b.at[t, me],
            send_sem=sb_sem.at[t, k],
            recv_sem=rb_sem.at[t, k],
            device_id=(after, other),
            device_id_type=MESH,
        )

    def copy_h(t):
        return pltpu.make_async_remote_copy(
            src_ref=state.at[t],
            dst_ref=held_h.at[t],
            send_sem=sh_sem.at[t],
            recv_sem=rh_sem.at[t],
            device_id=(after, me),
            device_id_type=MESH,
        )

    def own_a(t):
        return pltpu.make_async_copy(
            send_a.at[t, me // sharers], recv_a.at[t, me], own_sem.at[t]
        )

    far_first = sorted(range(1, peers), key=lambda k: -min(k, peers - k))

    def one_tick(t, first, last):
        hf = state[t].astype(jnp.float32)
        msq = jnp.mean(hf * hf, axis=-1, keepdims=True) + 1e-06
        normed = (hf * lax.rsqrt(msq) * gain_ref[...].astype(jnp.float32)).astype(jnp.bfloat16)
        slots = jnp.dot(pick[t], normed, preferred_element_type=jnp.float32)
        for j in range(held):
            send_a[t, j] = slots[j * MOST : (j + 1) * MOST].astype(jnp.bfloat16)
        for k in far_first:
            copy_a(t, k).start()
        own_a(t).start()
        copy_h(t).start()
        own_a(t).wait()
        for k in range(1, peers):
            copy_a(t, k).wait_recv()
        for p in range(peers):
            rows_f[p * MOST : (p + 1) * MOST, :] = recv_a[t, p].astype(jnp.float32)
        rows = rows_f[...].astype(jnp.bfloat16)

        @pl.when(t == 0)
        def _():
            for load in loads:
                load.wait()

        gate = nt_dot(rows, wg[...])
        upper = nt_dot(rows, wu[...])
        act = (gate / (1.0 + jnp.exp(-gate)) * upper).astype(jnp.bfloat16)
        y_f[...] = jnp.dot(act, wd[...], preferred_element_type=jnp.float32)
        for p in range(peers):
            send_b[t, p] = y_f[p * MOST : (p + 1) * MOST, :].astype(jnp.bfloat16)
        for k in far_first + [0]:
            copy_b(t, k).start()

        @pl.when(t == 0)
        def _():
            comb_copy.wait_recv()

        copy_h(t).wait_recv()
        for k in range(peers):
            copy_b(t, k).wait_recv()
        for p in range(peers):
            rows_f[p * MOST : (p + 1) * MOST, :] = recv_b[t, p].astype(jnp.float32)
        back = rows_f[...].astype(jnp.bfloat16)
        mix = comb_prev[t][:, : peers * MOST]
        out = held_h[t].astype(jnp.float32) + jnp.dot(
            mix, back, preferred_element_type=jnp.float32
        )
        state[t + 1] = out.astype(jnp.bfloat16)

    def body(t, carry):
        one_tick(t, None, None)
        return carry

    lax.fori_loop(0, ticks, body, 0)
    out_ref[...] = state[ticks]

    comb_copy.wait_send()

    def drain(t, carry):
        for k in range(1, peers):
            copy_a(t, k).wait_send()
        for k in range(peers):
            copy_b(t, k).wait_send()
        copy_h(t).wait_send()
        return carry

    lax.fori_loop(0, ticks, drain, 0)


def shards(sections, peers, hidden, route_ids, route_logits, norm_gain, w_gate, w_up, w_down):
    rows_dev, width = hidden.shape
    ticks = route_ids.shape[0]
    units = w_gate.shape[1]
    sharers = FE // units
    held = peers // sharers
    bf = jnp.bfloat16
    vmem = pl.BlockSpec(memory_space=pltpu.VMEM)
    hbm = pl.BlockSpec(memory_space=pl.ANY)
    dma = pltpu.SemaphoreType.DMA
    return pl.pallas_call(
        functools.partial(kernel, sections, peers, sharers),
        out_shape=jax.ShapeDtypeStruct((rows_dev, width), bf),
        in_specs=[vmem] * 4 + [hbm] * 3,
        out_specs=vmem,
        scratch_shapes=[
            pltpu.VMEM((units, width), bf),
            pltpu.VMEM((units, width), bf),
            pltpu.VMEM((units, width), bf),
            pltpu.VMEM((ticks + 1, rows_dev, width), bf),
            pltpu.VMEM((ticks, rows_dev, width), bf),
            pltpu.VMEM((ticks, held, MOST, width), bf),
            pltpu.VMEM((ticks, peers, MOST, width), bf),
            pltpu.VMEM((ticks, peers, MOST, width), bf),
            pltpu.VMEM((ticks, peers, MOST, width), bf),
            pltpu.VMEM((ticks, held * MOST, rows_dev), bf),
            pltpu.VMEM((ticks, rows_dev, 128), bf),
            pltpu.VMEM((ticks, rows_dev, 128), bf),
            pltpu.VMEM((peers * MOST, width), jnp.float32),
            pltpu.VMEM((peers * MOST, width), jnp.float32),
            dma((3,)),
            dma((ticks, peers)),
            dma((ticks, peers)),
            dma((ticks, peers)),
            dma((ticks, peers)),
            dma((ticks,)),
            dma((ticks,)),
            dma((2,)),
            dma((ticks,)),
        ],
        compiler_params=pltpu.CompilerParams(
            collective_id=0, has_side_effects=True, vmem_limit_bytes=56 * 1024 * 1024
        ),
    )(
        route_ids,
        route_logits,
        norm_gain,
        hidden,
        w_gate.reshape(units, width),
        w_up.reshape(units, width),
        w_down.reshape(units, width),
    )


def solution(mesh):
    placed = (
        P(("section", "ep"), None),
        P(None, ("section", "ep"), None),
        P(None, ("section", "ep"), None),
        P("section", None),
        P("section", "ep", None),
        P("section", "ep", None),
        P("section", "ep", None),
    )
    return jax.shard_map(
        functools.partial(shards, mesh.shape["section"], mesh.shape["ep"]),
        mesh=mesh,
        in_specs=placed,
        out_specs=P(("section", "ep"), None),
        check_vma=False,
    )
```

```python
import functools

import jax
import jax.numpy as jnp
from jax import lax
from jax.experimental import pallas as pl
from jax.experimental.pallas import tpu as pltpu
from jax.sharding import PartitionSpec as P

FE = 1536
MOST = 4
GROUPS = 2
MESH = pl.DeviceIdType.MESH


def nt_dot(rows, weight_t):
    return lax.dot_general(
        rows, weight_t, (((1,), (1,)), ((), ())), preferred_element_type=jnp.float32
    )


def kernel(
    sections,
    peers,
    sharers,
    ids_ref,
    logits_ref,
    gain_ref,
    hidden_ref,
    wg_hbm,
    wu_hbm,
    wd_hbm,
    out_ref,
    wg,
    wu,
    wd,
    state,
    held_h,
    send_a,
    recv_a,
    send_b,
    recv_b,
    pick,
    comb,
    comb_prev,
    rows_f,
    y_f,
    back_f,
    w_sem,
    sa_sem,
    ra_sem,
    sb_sem,
    rb_sem,
    sh_sem,
    rh_sem,
    c_sem,
):
    ticks, top, rows_dev = ids_ref.shape
    held = peers // sharers
    per_expert = sharers * MOST
    sec = lax.axis_index("section")
    me = lax.axis_index("ep")
    after = lax.rem(sec + 1, sections)
    before = lax.rem(sec + sections - 1, sections)

    loads = [
        pltpu.make_async_copy(src, dst, w_sem.at[i])
        for i, (src, dst) in enumerate(((wg_hbm, wg), (wu_hbm, wu), (wd_hbm, wd)))
    ]
    for load in loads:
        load.start()

    def ahead(k):
        return lax.rem(me + k, peers)

    def behind(k):
        return lax.rem(me + peers - k, peers)

    barrier = pltpu.get_barrier_semaphore()
    for k in range(peers):
        if k:
            pl.semaphore_signal(barrier, inc=1, device_id=(sec, ahead(k)), device_id_type=MESH)
        pl.semaphore_signal(barrier, inc=1, device_id=(before, ahead(k)), device_id_type=MESH)

    earlier = (
        lax.broadcasted_iota(jnp.int32, (rows_dev, rows_dev), 0)
        < lax.broadcasted_iota(jnp.int32, (rows_dev, rows_dev), 1)
    ).astype(jnp.bfloat16)
    eye = (
        lax.broadcasted_iota(jnp.int32, (rows_dev, rows_dev), 0)
        == lax.broadcasted_iota(jnp.int32, (rows_dev, rows_dev), 1)
    ).astype(jnp.bfloat16)

    def table(hit_rows, weight_rows, per):
        line = lax.broadcasted_iota(jnp.int32, (held * per, rows_dev), 0)
        hits = jnp.zeros((held * per, rows_dev), jnp.float32)
        weights = jnp.zeros((held * per, rows_dev), jnp.float32)
        for j in range(held):
            hits = jnp.where(line // per == j, hit_rows[j], hits)
            weights = jnp.where(line // per == j, weight_rows[j], weights)
        place = jnp.dot(hits.astype(jnp.bfloat16), earlier, preferred_element_type=jnp.float32)
        slot = lax.rem(line, MOST).astype(jnp.float32)
        chosen = jnp.where(place == slot, hits, 0.0)
        return chosen.astype(jnp.bfloat16), (
            chosen * weights.astype(jnp.bfloat16).astype(jnp.float32)
        ).astype(jnp.bfloat16)

    for t in range(ticks):
        ids = ids_ref[t]
        expo = jnp.exp(logits_ref[t])
        probs = expo / jnp.sum(expo, axis=0, keepdims=True)
        hit_rows = []
        weight_rows = []
        for j in range(held):
            match = ids == j
            hit_rows.append(jnp.sum(jnp.where(match, 1.0, 0.0), axis=0, keepdims=True))
            weight_rows.append(jnp.sum(jnp.where(match, probs, 0.0), axis=0, keepdims=True))
        pick[t] = table(hit_rows, weight_rows, MOST)[0]
        comb[t] = nt_dot(eye, table(hit_rows, weight_rows, per_expert)[1]).astype(jnp.bfloat16)

    state[0] = hidden_ref[...]
    pl.semaphore_wait(barrier, 2 * peers - 1)
    comb_copy = pltpu.make_async_remote_copy(
        src_ref=comb,
        dst_ref=comb_prev,
        send_sem=c_sem.at[0],
        recv_sem=c_sem.at[1],
        device_id=(after, me),
        device_id_type=MESH,
    )
    comb_copy.start()

    def copy_a(t, k):
        return pltpu.make_async_remote_copy(
            src_ref=send_a.at[t, ahead(k) // sharers],
            dst_ref=recv_a.at[t, k],
            send_sem=sa_sem.at[t, k],
            recv_sem=ra_sem.at[t, k],
            device_id=(sec, ahead(k)),
            device_id_type=MESH,
        )

    def copy_b(t, k):
        return pltpu.make_async_remote_copy(
            src_ref=send_b.at[t, k],
            dst_ref=recv_b.at[t, me],
            send_sem=sb_sem.at[t, k],
            recv_sem=rb_sem.at[t, me],
            device_id=(after, behind(k)),
            device_id_type=MESH,
        )

    def came_b(t, i):
        return pltpu.make_async_remote_copy(
            src_ref=send_b.at[t, i],
            dst_ref=recv_b.at[t, i],
            send_sem=sb_sem.at[t, i],
            recv_sem=rb_sem.at[t, i],
            device_id=(after, me),
            device_id_type=MESH,
        )

    def copy_h(t):
        return pltpu.make_async_remote_copy(
            src_ref=state.at[t],
            dst_ref=held_h.at[t],
            send_sem=sh_sem.at[t],
            recv_sem=rh_sem.at[t],
            device_id=(after, me),
            device_id_type=MESH,
        )

    turns = [
        sorted(range(g, peers, GROUPS), key=lambda k: -min(k, peers - k)) for g in range(GROUPS)
    ]

    def one_tick(t, carry):
        hf = state[t].astype(jnp.float32)
        msq = jnp.mean(hf * hf, axis=-1, keepdims=True) + 1e-06
        normed = (hf * lax.rsqrt(msq) * gain_ref[...].astype(jnp.float32)).astype(jnp.bfloat16)
        slots = jnp.dot(pick[t], normed, preferred_element_type=jnp.float32)
        for j in range(held):
            send_a[t, j] = slots[j * MOST : (j + 1) * MOST].astype(jnp.bfloat16)
        for turn in turns:
            for k in turn:
                if k:
                    copy_a(t, k).start()
        copy_h(t).start()

        for g, turn in enumerate(turns):
            for at, k in enumerate(turn):
                if k:
                    copy_a(t, k).wait_recv()
                mine = recv_a[t, k] if k else send_a[t, me // sharers]
                rows_f[g, at * MOST : (at + 1) * MOST, :] = mine.astype(jnp.float32)
            rows = rows_f[g].astype(jnp.bfloat16)
            if g == 0:

                @pl.when(t == 0)
                def _():
                    for load in loads:
                        load.wait()

            gate = nt_dot(rows, wg[...])
            upper = nt_dot(rows, wu[...])
            act = (gate / (1.0 + jnp.exp(-gate)) * upper).astype(jnp.bfloat16)
            y_f[g] = jnp.dot(act, wd[...], preferred_element_type=jnp.float32)
            for at, k in enumerate(turn):
                send_b[t, k] = y_f[g, at * MOST : (at + 1) * MOST, :].astype(jnp.bfloat16)
                copy_b(t, k).start()

        @pl.when(t == 0)
        def _():
            comb_copy.wait_recv()

        copy_h(t).wait_recv()
        for i in range(peers):
            came_b(t, i).wait_recv()
            back_f[i * MOST : (i + 1) * MOST, :] = recv_b[t, i].astype(jnp.float32)
        out = held_h[t].astype(jnp.float32) + jnp.dot(
            comb_prev[t], back_f[...].astype(jnp.bfloat16), preferred_element_type=jnp.float32
        )
        state[t + 1] = out.astype(jnp.bfloat16)
        return carry

    lax.fori_loop(0, ticks, one_tick, 0)
    out_ref[...] = state[ticks]

    comb_copy.wait_send()

    def drain(t, carry):
        for k in range(peers):
            if k:
                copy_a(t, k).wait_send()
            copy_b(t, k).wait_send()
        copy_h(t).wait_send()
        return carry

    lax.fori_loop(0, ticks, drain, 0)


def shards(sections, peers, hidden, route_ids, route_logits, norm_gain, w_gate, w_up, w_down):
    rows_dev, width = hidden.shape
    ticks = route_ids.shape[0]
    units = w_gate.shape[1]
    sharers = FE // units
    held = peers // sharers
    bf = jnp.bfloat16
    vmem = pl.BlockSpec(memory_space=pltpu.VMEM)
    hbm = pl.BlockSpec(memory_space=pl.ANY)
    dma = pltpu.SemaphoreType.DMA
    return pl.pallas_call(
        functools.partial(kernel, sections, peers, sharers),
        out_shape=jax.ShapeDtypeStruct((rows_dev, width), bf),
        in_specs=[vmem] * 4 + [hbm] * 3,
        out_specs=vmem,
        scratch_shapes=[
            pltpu.VMEM((units, width), bf),
            pltpu.VMEM((units, width), bf),
            pltpu.VMEM((units, width), bf),
            pltpu.VMEM((ticks + 1, rows_dev, width), bf),
            pltpu.VMEM((ticks, rows_dev, width), bf),
            pltpu.VMEM((ticks, held, MOST, width), bf),
            pltpu.VMEM((ticks, peers, MOST, width), bf),
            pltpu.VMEM((ticks, peers, MOST, width), bf),
            pltpu.VMEM((ticks, peers, MOST, width), bf),
            pltpu.VMEM((ticks, held * MOST, rows_dev), bf),
            pltpu.VMEM((ticks, rows_dev, peers * MOST), bf),
            pltpu.VMEM((ticks, rows_dev, peers * MOST), bf),
            pltpu.VMEM((GROUPS, peers // GROUPS * MOST, width), jnp.float32),
            pltpu.VMEM((GROUPS, peers // GROUPS * MOST, width), jnp.float32),
            pltpu.VMEM((peers * MOST, width), jnp.float32),
            dma((3,)),
            dma((ticks, peers)),
            dma((ticks, peers)),
            dma((ticks, peers)),
            dma((ticks, peers)),
            dma((ticks,)),
            dma((ticks,)),
            dma((2,)),
        ],
        compiler_params=pltpu.CompilerParams(
            collective_id=0, has_side_effects=True, vmem_limit_bytes=56 * 1024 * 1024
        ),
    )(
        jnp.swapaxes(route_ids, 1, 2),
        jnp.swapaxes(route_logits, 1, 2),
        norm_gain,
        hidden,
        w_gate.reshape(units, width),
        w_up.reshape(units, width),
        w_down.reshape(units, width),
    )


def solution(mesh):
    placed = (
        P(("section", "ep"), None),
        P(None, ("section", "ep"), None),
        P(None, ("section", "ep"), None),
        P("section", None),
        P("section", "ep", None),
        P("section", "ep", None),
        P("section", "ep", None),
    )
    return jax.shard_map(
        functools.partial(shards, mesh.shape["section"], mesh.shape["ep"]),
        mesh=mesh,
        in_specs=placed,
        out_specs=P(("section", "ep"), None),
        check_vma=False,
    )
```

```python
import functools

import jax
import jax.numpy as jnp
from jax import lax
from jax.experimental import pallas as pl
from jax.experimental.pallas import tpu as pltpu
from jax.sharding import PartitionSpec as P

FE = 1536
MOST = 4
GROUPS = 2
MESH = pl.DeviceIdType.MESH


def nt_dot(rows, weight_t):
    return lax.dot_general(
        rows, weight_t, (((1,), (1,)), ((), ())), preferred_element_type=jnp.float32
    )


def kernel(
    sections,
    peers,
    sharers,
    ids_ref,
    logits_ref,
    gain_ref,
    hidden_ref,
    wg_hbm,
    wu_hbm,
    wd_hbm,
    out_ref,
    wg,
    wu,
    wd,
    state,
    held_h,
    send_a,
    recv_a,
    send_b,
    recv_b,
    pick,
    comb,
    comb_prev,
    rows_f,
    y_f,
    back_f,
    w_sem,
    sa_sem,
    ra_sem,
    sb_sem,
    rb_sem,
    sh_sem,
    rh_sem,
    c_sem,
):
    ticks, top, rows_dev = ids_ref.shape
    held = peers // sharers
    sec = lax.axis_index("section")
    me = lax.axis_index("ep")
    after = lax.rem(sec + 1, sections)
    before = lax.rem(sec + sections - 1, sections)

    loads = [
        pltpu.make_async_copy(src, dst, w_sem.at[i])
        for i, (src, dst) in enumerate(((wg_hbm, wg), (wu_hbm, wu), (wd_hbm, wd)))
    ]
    for load in loads:
        load.start()

    def ahead(k):
        return lax.rem(me + k, peers)

    def behind(k):
        return lax.rem(me + peers - k, peers)

    barrier = pltpu.get_barrier_semaphore()
    for k in range(peers):
        if k:
            pl.semaphore_signal(barrier, inc=1, device_id=(sec, ahead(k)), device_id_type=MESH)
        pl.semaphore_signal(barrier, inc=1, device_id=(before, ahead(k)), device_id_type=MESH)

    earlier = (
        lax.broadcasted_iota(jnp.int32, (rows_dev, rows_dev), 0)
        < lax.broadcasted_iota(jnp.int32, (rows_dev, rows_dev), 1)
    ).astype(jnp.bfloat16)
    eye = (
        lax.broadcasted_iota(jnp.int32, (rows_dev, rows_dev), 0)
        == lax.broadcasted_iota(jnp.int32, (rows_dev, rows_dev), 1)
    ).astype(jnp.bfloat16)

    turns = [
        sorted(range(g, peers, GROUPS), key=lambda k: -min(k, peers - k)) for g in reversed(range(GROUPS))
    ]
    lines = peers // GROUPS * MOST

    def routing(t):
        ids = ids_ref[t]
        expo = jnp.exp(logits_ref[t])
        probs = expo / jnp.sum(expo, axis=0, keepdims=True)
        matches = [ids == j for j in range(held)]
        hit_rows = [jnp.sum(jnp.where(m, 1.0, 0.0), axis=0, keepdims=True) for m in matches]
        weight_rows = [jnp.sum(jnp.where(m, probs, 0.0), axis=0, keepdims=True) for m in matches]
        return hit_rows, weight_rows

    def choose(hit_rows, expert):
        shape = (expert.shape[0], rows_dev)
        hits = jnp.zeros(shape, jnp.float32)
        for j in range(held):
            hits = jnp.where(expert == j, hit_rows[j], hits)
        place = jnp.dot(hits.astype(jnp.bfloat16), earlier, preferred_element_type=jnp.float32)
        slot = lax.rem(lax.broadcasted_iota(jnp.int32, shape, 0), MOST).astype(jnp.float32)
        return jnp.where(place == slot, hits, 0.0)

    def make_pick(t):
        expert = lax.broadcasted_iota(jnp.int32, (held * MOST, rows_dev), 0) // MOST
        pick[t] = choose(routing(t)[0], expert).astype(jnp.bfloat16)

    def make_comb(t):
        hit_rows, weight_rows = routing(t)
        for g, turn in enumerate(turns):
            place = lax.broadcasted_iota(jnp.int32, (lines, rows_dev), 0) // MOST
            away = jnp.zeros((lines, rows_dev), jnp.int32)
            for at, k in enumerate(turn):
                away = jnp.where(place == at, k, away)
            expert = lax.rem(me + away, peers) // sharers
            weights = jnp.zeros((lines, rows_dev), jnp.float32)
            for j in range(held):
                weights = jnp.where(expert == j, weight_rows[j], weights)
            rounded = weights.astype(jnp.bfloat16).astype(jnp.float32)
            scaled = (choose(hit_rows, expert) * rounded).astype(jnp.bfloat16)
            comb[t, g] = nt_dot(eye, scaled).astype(jnp.bfloat16)

    make_pick(0)
    state[0] = hidden_ref[...]
    pl.semaphore_wait(barrier, 2 * peers - 1)
    comb_copy = pltpu.make_async_remote_copy(
        src_ref=comb,
        dst_ref=comb_prev,
        send_sem=c_sem.at[0],
        recv_sem=c_sem.at[1],
        device_id=(after, me),
        device_id_type=MESH,
    )

    def copy_a(t, k):
        return pltpu.make_async_remote_copy(
            src_ref=send_a.at[t, ahead(k) // sharers],
            dst_ref=recv_a.at[t, k],
            send_sem=sa_sem.at[t, k],
            recv_sem=ra_sem.at[t, k],
            device_id=(sec, ahead(k)),
            device_id_type=MESH,
        )

    def copy_b(t, k):
        return pltpu.make_async_remote_copy(
            src_ref=send_b.at[t, k],
            dst_ref=recv_b.at[t, k],
            send_sem=sb_sem.at[t, k],
            recv_sem=rb_sem.at[t, k],
            device_id=(after, behind(k)),
            device_id_type=MESH,
        )

    def copy_h(t):
        return pltpu.make_async_remote_copy(
            src_ref=state.at[t],
            dst_ref=held_h.at[t],
            send_sem=sh_sem.at[t],
            recv_sem=rh_sem.at[t],
            device_id=(after, me),
            device_id_type=MESH,
        )

    def one_tick(t, carry):
        hf = jnp.dot(pick[t], state[t], preferred_element_type=jnp.float32)
        msq = jnp.mean(hf * hf, axis=-1, keepdims=True) + 1e-06
        slots = hf * lax.rsqrt(msq) * gain_ref[...].astype(jnp.float32)
        for j in range(held):
            send_a[t, j] = slots[j * MOST : (j + 1) * MOST].astype(jnp.bfloat16)
        for turn in turns:
            for k in turn:
                if k:
                    copy_a(t, k).start()
        copy_h(t).start()

        @pl.when(t == 0)
        def _():
            for later in range(1, ticks):
                make_pick(later)
            for each in range(ticks):
                make_comb(each)
            comb_copy.start()

        for g, turn in enumerate(turns):
            for at, k in enumerate(turn):
                if k:
                    copy_a(t, k).wait_recv()
                mine = recv_a[t, k] if k else send_a[t, me // sharers]
                rows_f[g, at * MOST : (at + 1) * MOST, :] = mine.astype(jnp.float32)
            rows = rows_f[g].astype(jnp.bfloat16)
            if g == 0:

                @pl.when(t == 0)
                def _():
                    for load in loads:
                        load.wait()

            gate = nt_dot(rows, wg[...])
            upper = nt_dot(rows, wu[...])
            act = (gate / (1.0 + jnp.exp(-gate)) * upper).astype(jnp.bfloat16)
            y_f[g] = jnp.dot(act, wd[...], preferred_element_type=jnp.float32)
            for at, k in enumerate(turn):
                send_b[t, k] = y_f[g, at * MOST : (at + 1) * MOST, :].astype(jnp.bfloat16)
                copy_b(t, k).start()

        @pl.when(t == 0)
        def _():
            comb_copy.wait_recv()

        copy_h(t).wait_recv()
        out = held_h[t].astype(jnp.float32)
        for g, turn in enumerate(turns):
            for at, k in enumerate(turn):
                copy_b(t, k).wait_recv()
                back_f[g, at * MOST : (at + 1) * MOST, :] = recv_b[t, k].astype(jnp.float32)
            out = out + jnp.dot(
                comb_prev[t, g],
                back_f[g].astype(jnp.bfloat16),
                preferred_element_type=jnp.float32,
            )
        state[t + 1] = out.astype(jnp.bfloat16)
        return carry

    lax.fori_loop(0, ticks, one_tick, 0)
    out_ref[...] = state[ticks]

    comb_copy.wait_send()

    def drain(t, carry):
        for k in range(peers):
            if k:
                copy_a(t, k).wait_send()
            copy_b(t, k).wait_send()
        copy_h(t).wait_send()
        return carry

    lax.fori_loop(0, ticks, drain, 0)


def shards(sections, peers, hidden, route_ids, route_logits, norm_gain, w_gate, w_up, w_down):
    rows_dev, width = hidden.shape
    ticks = route_ids.shape[0]
    units = w_gate.shape[1]
    sharers = FE // units
    held = peers // sharers
    bf = jnp.bfloat16
    vmem = pl.BlockSpec(memory_space=pltpu.VMEM)
    hbm = pl.BlockSpec(memory_space=pl.ANY)
    dma = pltpu.SemaphoreType.DMA
    return pl.pallas_call(
        functools.partial(kernel, sections, peers, sharers),
        out_shape=jax.ShapeDtypeStruct((rows_dev, width), bf),
        in_specs=[vmem] * 4 + [hbm] * 3,
        out_specs=vmem,
        scratch_shapes=[
            pltpu.VMEM((units, width), bf),
            pltpu.VMEM((units, width), bf),
            pltpu.VMEM((units, width), bf),
            pltpu.VMEM((ticks + 1, rows_dev, width), bf),
            pltpu.VMEM((ticks, rows_dev, width), bf),
            pltpu.VMEM((ticks, held, MOST, width), bf),
            pltpu.VMEM((ticks, peers, MOST, width), bf),
            pltpu.VMEM((ticks, peers, MOST, width), bf),
            pltpu.VMEM((ticks, peers, MOST, width), bf),
            pltpu.VMEM((ticks, held * MOST, rows_dev), bf),
            pltpu.VMEM((ticks, GROUPS, rows_dev, peers // GROUPS * MOST), bf),
            pltpu.VMEM((ticks, GROUPS, rows_dev, peers // GROUPS * MOST), bf),
            pltpu.VMEM((GROUPS, peers // GROUPS * MOST, width), jnp.float32),
            pltpu.VMEM((GROUPS, peers // GROUPS * MOST, width), jnp.float32),
            pltpu.VMEM((GROUPS, peers // GROUPS * MOST, width), jnp.float32),
            dma((3,)),
            dma((ticks, peers)),
            dma((ticks, peers)),
            dma((ticks, peers)),
            dma((ticks, peers)),
            dma((ticks,)),
            dma((ticks,)),
            dma((2,)),
        ],
        compiler_params=pltpu.CompilerParams(
            collective_id=0, has_side_effects=True, vmem_limit_bytes=56 * 1024 * 1024
        ),
    )(
        jnp.swapaxes(route_ids, 1, 2),
        jnp.swapaxes(route_logits, 1, 2),
        norm_gain,
        hidden,
        w_gate.reshape(units, width),
        w_up.reshape(units, width),
        w_down.reshape(units, width),
    )


def solution(mesh):
    placed = (
        P(("section", "ep"), None),
        P(None, ("section", "ep"), None),
        P(None, ("section", "ep"), None),
        P("section", None),
        P("section", "ep", None),
        P("section", "ep", None),
        P("section", "ep", None),
    )
    return jax.shard_map(
        functools.partial(shards, mesh.shape["section"], mesh.shape["ep"]),
        mesh=mesh,
        in_specs=placed,
        out_specs=P(("section", "ep"), None),
        check_vma=False,
    )
```
